32 devices in a mesh: zone: 8 (over z, x), tile: 4 (over y, core).
Axes of the slice: x: 2, y: 2, z: 4, core: 2. Of those that a mesh axis runs over, the one named last changes fastest.
Arguments:
- a_coord: float32 [2, 1048576], P(None, ('zone', 'tile')), may hold values from -6 to 6
- a_var: float32 [1048576], P(('zone', 'tile')), may hold values from 0.1 to 1
- dest: int32 [8192, 1], P(('zone', 'tile')), may hold values from 0 to 31; in each aligned block of 256 rows (0 to 255, 256 to 511, ...) at most 16 rows name the same one
- cand: int32 [8192, 4], P(('zone', 'tile')), may hold values from 0 to 79
- cand_count: int32 [8192, 1], P(('zone', 'tile')), may hold values from 1 to 4
- b_coord: float32 [2, 262144], P(None, ('zone', 'tile')), may hold values from -6 to 6
- b_var: float32 [262144], P(('zone', 'tile')), may hold values from 0.1 to 1
- b_prior: float32 [262144], P(('zone', 'tile')), may hold values from 0.002 to 0.02
- b_flux: float32 [3, 262144], P(None, ('zone', 'tile')), may hold values from -6 to 6
Outputs:
- matched: float32 [5, 1048576], P(None, ('zone', 'tile'))
- match_prob: float32 [1048576], P(('zone', 'tile'))
The draws below stay inside these ranges and needn't reach their ends.
Inputs may be any that keep to these rules, and one draw needn't show every extreme that they name: `dest`: among the 256 blocks of one device, at most 16 name any one owner device, a bound that some block reaches.
All inputs are finite; a program needn't handle non-finite values.
Results may differ from the reference program's by a relative error of at most 0.0003.
Values sent between devices are 32-bit elements; how exact they have to be, the bound alone decides.
No kernel may reach another device: no remote copies, remote signals or barrier semaphores. Data moves between devices by JAX's collectives and lax.ppermute only.
A program may use at most 64 MiB of HBM per device.

```python
import math
import jax
import jax.numpy as jnp
import numpy as np
from jax import lax

TB = 128
F = 3
K = 4
NB_B = 64
MB = 8
BA = 256
CAP = 16
NW = 80
A_BLOCKS = 8192
A_ROWS = 1048576
B_ROWS = 262144
N_ZONE = 8
N_TILE = 4
DEVICES = 32


def with_ends(values, key, smallest, top_value):
    place = [jax.random.randint(jax.random.fold_in(key, axis), (), 0, length) for axis, length in enumerate(values.shape)]
    longest = values.shape.index(max(values.shape))
    neighbour = place[:longest] + [(place[longest] + 1) % values.shape[longest]] + place[longest + 1:]
    return values.at[tuple(place)].set(smallest).at[tuple(neighbour)].set(top_value)


def level_of(key, dims, cuts, smallest, high):
    def one(dim, shards_of):
        steps = jax.random.uniform(jax.random.fold_in(jax.random.fold_in(key, 6), dim), (shards_of,), jnp.float32, smallest / len(cuts), high / len(cuts))
        return jnp.repeat(jnp.exp(steps), dims[dim] // shards_of).reshape((-1,) + (1,) * (len(dims) - dim - 1))

    gain = one(*cuts[0])
    for cut in cuts[1:]:
        gain = gain * one(*cut)
    return gain


def deal_out(stream_key, own, number, rows, count, top, limit, slope):
    sequence = jax.random.permutation(stream_key, count)
    heavy_load, common = load_shares(count, rows * top, limit, slope, True), load_shares(count, rows * top, limit, slope, False)
    places = jnp.arange(count)

    def named(lengths, turn):
        used = int((lengths > 0).sum())
        fixed = max(1, used // 4)
        moved = fixed + (places - fixed + turn * (used - fixed)) % max(1, count - fixed)
        return jnp.zeros((count,), jnp.int32).at[sequence[jnp.where(places < fixed, places, moved)]].set(jnp.asarray(lengths, jnp.int32))

    lengths = jnp.where(number % 4 == 0, named(heavy_load, number // 4), named(common, number - number // 4 - 1))
    mixed = jax.random.permutation(jax.random.fold_in(own, 3), count)
    donor, taker = mixed[0:count // 2 * 2:2], mixed[1:count // 2 * 2:2]
    room = jnp.minimum(lengths[donor] - 1, limit - lengths[taker]) // 2
    room = jnp.where((donor == sequence[0]) | (taker == sequence[0]) | (lengths[taker] == 0), 0, jnp.maximum(room, 0))
    moved = jax.random.randint(jax.random.fold_in(own, 4), (count // 2,), 0, 1 << 20) % (room + 1)
    lengths = lengths.at[donor].add(-moved).at[taker].add(moved)
    members = jnp.searchsorted(jnp.cumsum(lengths), jnp.arange(rows * top), side="right").astype(jnp.int32)
    table = members.reshape(top, rows).T
    table = table[jax.random.permutation(jax.random.fold_in(own, 1), rows)]
    turn = jax.random.randint(jax.random.fold_in(own, 2), (rows, 1), 0, top)
    return jnp.take_along_axis(table, (jnp.arange(top)[None, :] + turn) % top, axis=1)


def load_shares(count, total, most, lean, full):
    portions = [(1 << 20) // math.isqrt(grade ** lean) + 1 for grade in range(1, count + 1)]
    largest = most if full else min(most, max(-(-total // count), total * portions[0] // sum(portions)))
    least = 1 if total - largest >= count - 1 else 0
    holding, spare = [largest] + [least] * (count - 1), total - largest - least * (count - 1)
    while spare > 0:
        free = [i for i in range(1, count) if holding[i] < largest] or [i for i in range(1, count) if holding[i] < most]
        whole, budget = sum([portions[i] for i in free]), spare
        for i in free:
            more = min(most - holding[i], max(1, budget * portions[i] // whole), spare)
            holding[i] = holding[i] + more
            spare = spare - more
    return np.array(holding)


def centred(key, extent, scale, reach, cuts=(), kind=jnp.bfloat16):
    array = scale * jax.random.normal(key, extent, jnp.float32)
    if cuts:
        array = array * level_of(key, extent, cuts, -0.22, 0.18)
    return jnp.clip(array, -reach, reach).astype(kind)


def setup_inputs(seed: int = 0) -> dict:
    splits = jax.random.split(jax.random.key(seed), 10)
    a_coord = centred(splits[0], (2, A_ROWS), 1.0, 6.0, ((1, 32),), jnp.float32)
    a_var = jnp.clip(jnp.exp(math.log(1.0) - 2.3025851 * jax.random.uniform(splits[1], (A_ROWS,), jnp.float32) ** level_of(splits[1], (A_ROWS,), ((0, 32),), -0.2, 0.2)), 0.1, 1.0)
    dest_keys = jax.random.split(jax.random.fold_in(splits[2], 1), A_BLOCKS // BA)
    dest_turns = jax.random.permutation(jax.random.fold_in(splits[2], 3), A_BLOCKS // BA)
    dest = jax.vmap(lambda own, number: deal_out(jax.random.fold_in(splits[2], 2), own, number, BA, DEVICES, 1, CAP, 2))(dest_keys, dest_turns).reshape((A_BLOCKS, 1))
    cand = with_ends(jax.random.randint(splits[3], (A_BLOCKS, K), 0, NW), jax.random.fold_in(splits[3], 1), 0, NW - 1).astype(jnp.int32)
    cand_count = with_ends(jax.random.randint(splits[4], (A_BLOCKS, 1), 1, K + 1), jax.random.fold_in(splits[4], 1), 1, K).astype(jnp.int32)
    b_coord = centred(splits[5], (2, B_ROWS), 1.0, 6.0, ((1, 32),), jnp.float32)
    b_var = jnp.clip(jnp.exp(math.log(1.0) - 2.3025851 * jax.random.uniform(splits[6], (B_ROWS,), jnp.float32) ** level_of(splits[6], (B_ROWS,), ((0, 32),), -0.2, 0.2)), 0.1, 1.0)
    b_prior = jnp.clip(jnp.exp(math.log(0.02) - 2.30258502 * jax.random.uniform(splits[7], (B_ROWS,), jnp.float32) ** level_of(splits[7], (B_ROWS,), ((0, 32),), -0.2, 0.2)), 0.002, 0.02)
    b_flux = centred(splits[8], (F, B_ROWS), 1.0, 6.0, ((1, 32),), jnp.float32)
    return dict(a_coord=a_coord, a_var=a_var, dest=dest, cand=cand, cand_count=cand_count, b_coord=b_coord, b_var=b_var, b_prior=b_prior, b_flux=b_flux)


def slot_match(a_block, candidates, live_count):
    numerator = jnp.zeros((5, a_block.shape[1]), jnp.float32)
    weight_sum = jnp.zeros((a_block.shape[1],), jnp.float32)
    for position in range(len(candidates)):
        block_data = candidates[position]
        is_live = jnp.where(live_count > position, 1.0, 0.0).astype(jnp.float32)
        delta_u = a_block[0][:, None] - block_data[0][None, :]
        delta_v = a_block[1][:, None] - block_data[1][None, :]
        var_sum = a_block[2][:, None] + block_data[5][None, :]
        weight = (block_data[6] * is_live)[None, :] * (2.0 / var_sum) * jnp.exp(-(delta_u * delta_u + delta_v * delta_v) / (2.0 * var_sum))
        numerator = numerator + jnp.einsum("fj,ij->fi", block_data[:5], weight, precision=lax.Precision.HIGHEST)
        weight_sum = weight_sum + jnp.sum(weight, axis=1)
    inverse = 1.0 / (1.0 + weight_sum)
    return jnp.concatenate([numerator * inverse[None, :], (weight_sum * inverse)[None, :]], axis=0)


def reference(a_coord, a_var, dest, cand, cand_count, b_coord, b_var, b_prior, b_flux):
    devices = N_ZONE * N_TILE
    b_stack = jnp.concatenate([b_coord, b_flux, b_var[None, :], b_prior[None, :]], axis=0)
    b_blocks = b_stack.reshape(7, devices * NB_B, TB).transpose(1, 0, 2)
    a_stack = jnp.concatenate([a_coord, a_var[None, :]], axis=0)
    a_blocks = a_stack.reshape(3, A_BLOCKS, TB).transpose(1, 0, 2)

    def match_block(items):
        a_block, target, names, live_count = items
        zone_row = target // N_TILE
        candidates = []
        for position in range(K):
            window_pos = names[position]
            lower_block = (target - N_TILE) * NB_B + NB_B - MB + window_pos
            own_block = target * NB_B + window_pos - MB
            upper_block = (target + N_TILE) * NB_B + window_pos - MB - NB_B
            chosen = jnp.where(window_pos < MB, lower_block, jnp.where(window_pos < MB + NB_B, own_block, upper_block))
            valid = jnp.where(window_pos < MB, zone_row > 0, jnp.where(window_pos < MB + NB_B, True, zone_row < N_ZONE - 1))
            chosen = jnp.clip(chosen, 0, devices * NB_B - 1).astype(jnp.int32)
            candidates.append(b_blocks[chosen] * valid.astype(jnp.float32))
        return slot_match(a_block, candidates, live_count)

    results = lax.map(match_block, (a_blocks, dest[:, 0], cand, cand_count[:, 0]), batch_size=256)
    results = results.transpose(1, 0, 2).reshape(6, A_ROWS)
    return results[:5], results[5]
```

```python
import functools
import math

import jax
import jax.numpy as jnp
from jax import lax
from jax.experimental import pallas as pl
from jax.experimental.pallas import tpu as pltpu
from jax.sharding import PartitionSpec as P

TB = 128
MB = 8
NQ = 7
VAR, PRIOR = 5, 6
UNROLL = 16
BF, F32 = jnp.bfloat16, jnp.float32
HALF_LOG2E = 0.5 * math.log2(math.e)
AXES = ("zone", "tile")
VMEM = pl.BlockSpec(memory_space=pltpu.VMEM)
SMEM = pl.BlockSpec(memory_space=pltpu.SMEM)
ANY = pl.BlockSpec(memory_space=pl.ANY)


def split3(x):
    high = x.astype(BF).astype(F32)
    middle = (x - high).astype(BF).astype(F32)
    return high, middle, x - high - middle


def is_grid(mesh_shape):
    return mesh_shape["zone"] % 2 == 0 and mesh_shape["tile"] == 4


class Grid:
    def __init__(self, zones, tiles):
        self.zones, self.tiles, self.high = zones, tiles, zones // 2

    def perm(self, move):
        pairs = []
        for d in range(self.zones * self.tiles):
            zone, tile = divmod(d, self.tiles)
            h, x, y, c = move(zone // 2, zone % 2, tile // 2, tile % 2)
            pairs.append((d, ((h % self.high) * 2 + x) * self.tiles + y * 2 + c))
        return pairs

    def ring(self):
        return self.perm(lambda h, x, y, c: (h + 1, x, y, c))

    def side(self, first):
        return self.perm(lambda h, x, y, c: (h, x ^ 1, y, c) if (c == 0) == first else (h, x, y ^ 1, c))

    def core(self):
        return self.perm(lambda h, x, y, c: (h, x, y, c ^ 1))


def gather_phases(own, grid):
    phases = []
    held = own
    for step in range(grid.high):
        later = lax.ppermute(held, AXES, grid.ring()) if step < grid.high - 1 else None
        pair = jnp.concatenate([held, lax.ppermute(held, AXES, grid.side(True))], axis=0)
        four = jnp.concatenate([pair, lax.ppermute(pair, AXES, grid.side(False))], axis=0)
        phases.append((four, lax.ppermute(four, AXES, grid.core())))
        held = later
    return phases


def locate(zone, tile, block, grid, rows):
    my_zone, my_tile = lax.axis_index("zone"), lax.axis_index("tile")
    phase = lax.rem((my_zone >> 1) - (zone >> 1) + grid.high, grid.high)
    dx = (zone & 1) ^ (my_zone & 1)
    dy = ((tile >> 1) ^ (my_tile >> 1)) & 1
    dc = (tile ^ my_tile) & 1
    odd = tile & 1
    place = jnp.where(odd == 0, dx + 2 * dy, dy + 2 * dx)
    return phase, (4 * dc + place) * rows + block


def plan_kernel(items, phases, length, dummy, entry_ref, codes_ref, count_ref):
    def step(i, counts):
        for t in range(4):
            entry = entry_ref[i * 4 + t]
            phase, code = entry >> 26, entry & ((1 << 26) - 1)
            place = counts[phases]
            start = phases * length
            for p in reversed(range(phases)):
                place = jnp.where(phase == p, counts[p], place)
            codes_ref[phase * length + place] = code
            counts = tuple(c + jnp.where(phase == p, 1, 0) for p, c in enumerate(counts))
        return counts

    counts = lax.fori_loop(0, items // 4, step, (jnp.int32(0),) * (phases + 1))
    for p in range(phases):
        for t in range(UNROLL):
            codes_ref[p * length + counts[p] + t] = jnp.int32(dummy)
        count_ref[p] = counts[p]


def prep_kernel(blocks, coord_ref, var_ref, at_ref):
    eye = jnp.where(
        lax.broadcasted_iota(jnp.int32, (TB, TB), 0) == lax.broadcasted_iota(jnp.int32, (TB, TB), 1), 1.0, 0.0
    ).astype(BF)
    row = lax.broadcasted_iota(jnp.int32, (8, TB), 0)

    def step(i, _):
        for t in range(8):
            block = i * 8 + t
            lanes = pl.ds(pl.multiple_of(block * TB, TB), TB)
            u, v = coord_ref[0:1, lanes], coord_ref[1:2, lanes]
            s = var_ref[pl.ds(block, 1), :]
            q = -HALF_LOG2E * (u * u + v * v)
            tile = jnp.where(row == 3, q, jnp.where(row == 4, s, jnp.where(row == 2, 1.0, 0.0)))
            tile = jnp.where(row == 0, u, jnp.where(row == 1, v, tile))
            h, m, l = split3(tile)
            stack = jnp.concatenate([h, h, m, m, h, l], axis=0).astype(BF)
            turned = lax.dot_general(eye, stack, (((1,), (1,)), ((), ())), preferred_element_type=F32)
            at_ref[lanes, :] = turned.astype(BF)
        return 0

    lax.fori_loop(0, blocks // 8, step, 0)


def match_items(codes_ref, first, count, spacing, at_ref, b_ref, acc_ref):
    row = lax.broadcasted_iota(jnp.int32, (8, TB), 0)

    def step(i, _):
        sums = []
        for t in range(UNROLL):
            code = codes_ref[first + i * UNROLL + t]
            block, start = code >> 16, code & 0xFFFF
            x = b_ref[pl.ds(start, 8, stride=spacing), :]
            u, v, s, p = x[0:1], x[1:2], x[VAR : VAR + 1], x[PRIOR : PRIOR + 1]
            q = -HALF_LOG2E * (u * u + v * v)
            near = jnp.where(row == 2, q, jnp.where(row == 3, 1.0, 0.0))
            near = jnp.where(row < 2, x * (2 * HALF_LOG2E), near)
            spread = jnp.where(row == 2, s, jnp.where(row == 4, 1.0, 0.0))
            h, m, l = split3(jnp.concatenate([near, spread], axis=1))
            stack = jnp.concatenate([h, m, h, m, l, h], axis=0).astype(BF)
            held = jnp.minimum(block, at_ref.shape[0] // TB - 1)
            a = at_ref[pl.ds(pl.multiple_of(held * TB, TB), TB), :]
            both = jnp.dot(a, stack, preferred_element_type=F32)
            r = 1.0 / both[:, TB:]
            w = r * jnp.exp2(both[:, :TB] * r)
            w_high = w.astype(BF)
            w_low = (w - w_high.astype(F32)).astype(BF)
            f = jnp.where(row == VAR, 1.0, x) * (2.0 * p)
            f_high = f.astype(BF).astype(F32)
            f_low = f - f_high
            left = jnp.concatenate(
                [
                    jnp.concatenate([f_high, f_high], axis=1),
                    jnp.concatenate([f_low, jnp.zeros_like(f_low)], axis=1),
                ],
                axis=0,
            ).astype(BF)
            right = jnp.concatenate([w_high, w_low], axis=1)
            o = lax.dot_general(left, right, (((1,), (1,)), ((), ())), preferred_element_type=F32)
            sums.append((block, o[0:8] + o[8:16]))
        for block, o in sums:
            acc_ref[block] += o
        return 0

    lax.fori_loop(0, lax.div(count + (UNROLL - 1), jnp.int32(UNROLL)), step, 0)


def match_kernel(blocks, length, spacing, parts, codes_ref, count_ref, at_ref, *refs):
    chunks, (out_ref, prob_ref, b_ref, acc_ref, sems) = refs[: -5], refs[-5:]
    phases = len(chunks) // parts
    rows = chunks[0].shape[0]
    copies = [
        pltpu.make_async_copy(
            chunk, b_ref.at[i // parts, pl.ds((i % parts) * rows, rows), :], sems.at[i]
        )
        for i, chunk in enumerate(chunks)
    ]
    for copy in copies:
        copy.start()
    acc_ref[...] = jnp.zeros_like(acc_ref)
    for p in range(phases):
        b_ref[p, pl.ds(parts * rows, b_ref.shape[1] - parts * rows), :] = jnp.zeros(
            (b_ref.shape[1] - parts * rows, TB), F32
        )
    for copy in copies:
        copy.wait()
    for p in range(phases):
        match_items(codes_ref, p * length, count_ref[p], spacing, at_ref, b_ref.at[p], acc_ref)

    def finish(i, _):
        for t in range(8):
            block = i * 8 + t
            a = acc_ref[block]
            s = a[5:6]
            inverse = 1.0 / (1.0 + s)
            out_ref[:, pl.ds(pl.multiple_of(block * TB, TB), TB)] = (a * inverse)[0:5]
            prob_ref[pl.ds(block, 1), :] = s * inverse
        return 0

    lax.fori_loop(0, blocks // 8, finish, 0)


def body(a_coord, a_var, dest, cand, cand_count, b_coord, b_var, b_prior, b_flux):
    zones, tiles = lax.axis_size("zone"), lax.axis_size("tile")
    blocks = dest.shape[0]
    slots = cand.shape[1]
    own_blocks = b_var.shape[0] // TB
    rows = NQ * own_blocks
    fast = is_grid({"zone": zones, "tile": tiles})
    grid = Grid(zones, tiles)

    shift = (cand >= MB).astype(jnp.int32) + (cand >= MB + own_blocks).astype(jnp.int32) - 1
    zone = dest // tiles + shift
    tile = dest % tiles
    block = cand - MB - shift * own_blocks
    live = (jnp.arange(slots, dtype=jnp.int32)[None, :] < cand_count) & (zone >= 0) & (zone < zones)
    if fast:
        phases = grid.high
        phase, row = locate(zone, tile, block, grid, rows)
    else:
        phases = 1
        phase, row = jnp.zeros_like(zone), (zone * tiles + tile) * rows + block
    here = jnp.arange(blocks, dtype=jnp.int32)[:, None]
    entry = jnp.where(live, (phase << 26) | (here << 16) | row, phases << 26)
    items = blocks * slots
    length = items + UNROLL
    codes, counts = pl.pallas_call(
        functools.partial(plan_kernel, items, phases, length, blocks << 16),
        out_shape=(
            jax.ShapeDtypeStruct(((phases + 1) * length,), jnp.int32),
            jax.ShapeDtypeStruct((8,), jnp.int32),
        ),
        in_specs=[SMEM],
        out_specs=(SMEM, SMEM),
        name="plan",
    )(entry.T.reshape(-1))

    var_rows = a_var.reshape(blocks, TB)
    at = pl.pallas_call(
        functools.partial(prep_kernel, blocks),
        out_shape=jax.ShapeDtypeStruct((blocks * TB, 48), BF),
        in_specs=[VMEM, VMEM],
        out_specs=VMEM,
        name="prep",
    )(a_coord, var_rows)

    own = jnp.concatenate([b_coord, b_flux, b_var[None, :], b_prior[None, :]], axis=0).reshape(rows, TB)
    if fast:
        chunks = [c for pair in gather_phases(own, grid) for c in pair]
        parts = 2
    else:
        chunks = [lax.all_gather(own, AXES, axis=0, tiled=True)]
        parts = 1
    buffer_rows = parts * chunks[0].shape[0] + own_blocks
    matched, prob = pl.pallas_call(
        functools.partial(match_kernel, blocks, length, own_blocks, parts),
        out_shape=(
            jax.ShapeDtypeStruct((5, blocks * TB), F32),
            jax.ShapeDtypeStruct((blocks, TB), F32),
        ),
        in_specs=[SMEM, SMEM, VMEM] + [ANY] * len(chunks),
        out_specs=(VMEM, VMEM),
        scratch_shapes=[
            pltpu.VMEM((len(chunks) // parts, buffer_rows, TB), F32),
            pltpu.VMEM((blocks + 1, 8, TB), F32),
            pltpu.SemaphoreType.DMA((len(chunks),)),
        ],
        name="match",
    )(codes, counts, at, *chunks)
    return matched, prob.reshape(-1)


def solution(mesh):
    placed = (
        P(None, AXES),
        P(AXES),
        P(AXES, None),
        P(AXES, None),
        P(AXES, None),
        P(None, AXES),
        P(AXES),
        P(AXES),
        P(None, AXES),
    )
    return jax.shard_map(
        body, mesh=mesh, in_specs=placed, out_specs=(P(None, AXES), P(AXES)), check_vma=False
    )
```

```python
import functools
import math

import jax
import jax.numpy as jnp
from jax import lax
from jax.experimental import pallas as pl
from jax.experimental.pallas import tpu as pltpu
from jax.sharding import PartitionSpec as P


TB = 128
MB = 8
NQ = 7
VAR, PRIOR = 5, 6
UNROLL = 32
BF, F32 = jnp.bfloat16, jnp.float32
HALF_LOG2E = 0.5 * math.log2(math.e)
AXES = ("zone", "tile")
VMEM = pl.BlockSpec(memory_space=pltpu.VMEM)
SMEM = pl.BlockSpec(memory_space=pltpu.SMEM)


def params(mib):
    return pltpu.CompilerParams(vmem_limit_bytes=mib << 20)


def split3(x):
    high = x.astype(BF).astype(F32)
    middle = (x - high).astype(BF).astype(F32)
    return high, middle, x - high - middle


def is_grid(mesh_shape):
    return mesh_shape["zone"] % 2 == 0 and mesh_shape["tile"] == 4


class Grid:
    def __init__(self, zones, tiles):
        self.zones, self.tiles, self.high = zones, tiles, zones // 2

    def perm(self, move):
        pairs = []
        for d in range(self.zones * self.tiles):
            zone, tile = divmod(d, self.tiles)
            h, x, y, c = move(zone // 2, zone % 2, tile // 2, tile % 2)
            pairs.append((d, ((h % self.high) * 2 + x) * self.tiles + y * 2 + c))
        return pairs

    def shift(self, by):
        return self.perm(lambda h, x, y, c: (h + by, x, y, c))

    def side(self, first):
        return self.perm(lambda h, x, y, c: (h, x ^ 1, y, c) if (c == 0) == first else (h, x, y ^ 1, c))

    def core(self):
        return self.perm(lambda h, x, y, c: (h, x, y, c ^ 1))


def send(array, pairs):
    return lax.ppermute(array, AXES, pairs)


def gather_phases(own, grid):
    n = grid.high
    held = {0: own}
    order = [0]
    for step in range(1, n // 2 + 1):
        for s, back in ((step, 1), (n - step, -1)):
            if s not in held:
                held[s] = send(held[(s - back) % n], grid.shift(back))
                order.append(s)
    phases = []
    for s in order:
        z = held[s]
        pair = jnp.concatenate([z, send(z, grid.side(True))], axis=0)
        four = jnp.concatenate([pair, send(pair, grid.side(False))], axis=0)
        phases.append((four, send(four, grid.core())))
    return phases, order


def locate(zone, tile, block, grid, rows):
    my_zone, my_tile = lax.axis_index("zone"), lax.axis_index("tile")
    distance = lax.rem((my_zone >> 1) - (zone >> 1) + grid.high, grid.high)
    dx = (zone & 1) ^ (my_zone & 1)
    dy = ((tile >> 1) ^ (my_tile >> 1)) & 1
    dc = (tile ^ my_tile) & 1
    place = jnp.where((tile & 1) == 0, dx + 2 * dy, dy + 2 * dx)
    return distance, (dc << 16) | (place * rows + block)


def plan_kernel(phases, length, dummy, entry_ref, codes_ref, count_ref, place_ref, work_ref, sem):
    entry = entry_ref[...]
    high = entry.shape[0]
    phase = entry >> 27
    lanes = (TB, TB)
    earlier = lax.broadcasted_iota(jnp.int32, lanes, 0) < lax.broadcasted_iota(jnp.int32, lanes, 1)
    sums = jnp.concatenate([jnp.where(earlier, 1.0, 0.0), jnp.ones(lanes, F32)], axis=1).astype(BF)
    above = lax.broadcasted_iota(jnp.int32, (high, high), 1) < lax.broadcasted_iota(jnp.int32, (high, high), 0)
    above = jnp.where(above, 1.0, 0.0).astype(BF)
    place = phase * length
    totals = []
    for p in range(phases + 1):
        member = jnp.where(phase == p, 1.0, 0.0)
        both = jnp.dot(member.astype(BF), sums, preferred_element_type=F32)
        before, total = both[:, :TB], both[:, TB:]
        rows = jnp.dot(above, total.astype(BF), preferred_element_type=F32)
        place = place + jnp.where(phase == p, (before + rows).astype(jnp.int32), 0)
        totals.append(jnp.sum(total, axis=0, keepdims=True).astype(jnp.int32))
    place_ref[pl.ds(0, high), :] = place
    place_ref[pl.ds(high, high), :] = entry & ((1 << 27) - 1)
    place_ref[pl.ds(2 * high, 8), :] = jnp.concatenate(
        totals + [jnp.zeros((1, TB), jnp.int32)] * (7 - phases), axis=0
    )
    copy = pltpu.make_async_copy(place_ref, work_ref, sem)
    copy.start()
    copy.wait()

    def row(r, _):
        def step(i, _):
            for t in range(16):
                codes_ref[work_ref[r, i * 16 + t]] = work_ref[high + r, i * 16 + t]
            return 0

        return lax.fori_loop(0, TB // 16, step, 0)

    lax.fori_loop(0, high, row, 0)
    for p in range(phases):
        count = work_ref[2 * high + p, 0]
        for t in range(UNROLL):
            codes_ref[p * length + count + t] = jnp.int32(dummy)
        count_ref[p] = count


def prep_kernel(blocks, coord_ref, var_ref, at_ref):
    eye = jnp.where(
        lax.broadcasted_iota(jnp.int32, (TB, TB), 0) == lax.broadcasted_iota(jnp.int32, (TB, TB), 1), 1.0, 0.0
    ).astype(BF)
    row = lax.broadcasted_iota(jnp.int32, (8, TB), 0)

    def step(i, _):
        for t in range(8):
            block = i * 8 + t
            lanes = pl.ds(pl.multiple_of(block * TB, TB), TB)
            u, v = coord_ref[0:1, lanes], coord_ref[1:2, lanes]
            s = var_ref[pl.ds(block, 1), :]
            q = -HALF_LOG2E * (u * u + v * v)
            tile = jnp.where(row == 3, q, jnp.where(row == 4, s, jnp.where(row == 2, 1.0, 0.0)))
            tile = jnp.where(row == 0, u, jnp.where(row == 1, v, tile))
            h, m, l = split3(tile)
            stack = jnp.concatenate([h, h, m, m, h, l], axis=0).astype(BF)
            turned = lax.dot_general(eye, stack, (((1,), (1,)), ((), ())), preferred_element_type=F32)
            at_ref[lanes, :] = turned.astype(BF)
        return 0

    lax.fori_loop(0, blocks // 8, step, 0)


def match_items(codes_ref, first, count, spacing, at_ref, b_refs, acc_ref):
    row = lax.broadcasted_iota(jnp.int32, (8, TB), 0)
    gap = jnp.zeros((8 - NQ, TB), F32)

    def step(i, _):
        sums = []
        for t in range(UNROLL):
            code = codes_ref[first + i * UNROLL + t]
            block, half, start = code >> 17, (code >> 16) & 1, code & 0xFFFF
            x = b_refs[0][pl.ds(start, NQ, stride=spacing), :]
            if len(b_refs) > 1:
                x = jnp.where(half == 1, b_refs[1][pl.ds(start, NQ, stride=spacing), :], x)
            x = jnp.concatenate([x, gap], axis=0)
            u, v, s, p = x[0:1], x[1:2], x[VAR : VAR + 1], x[PRIOR : PRIOR + 1]
            q = -HALF_LOG2E * (u * u + v * v)
            near = jnp.where(row == 2, q, jnp.where(row == 3, 1.0, 0.0))
            near = jnp.where(row < 2, x * (2 * HALF_LOG2E), near)
            spread = jnp.where(row == 2, s, jnp.where(row == 4, 1.0, 0.0))
            h, m, l = split3(jnp.concatenate([near, spread], axis=1))
            stack = jnp.concatenate([h, m, h, m, l, h], axis=0).astype(BF)
            held = jnp.minimum(block, at_ref.shape[0] // TB - 1)
            a = at_ref[pl.ds(pl.multiple_of(held * TB, TB), TB), :]
            both = jnp.dot(a, stack, preferred_element_type=F32)
            r = 1.0 / both[:, TB:]
            w = r * jnp.exp2(both[:, :TB] * r)
            w_high = w.astype(BF)
            w_low = (w - w_high.astype(F32)).astype(BF)
            f = jnp.where(row == VAR, 1.0, x) * (2.0 * p)
            f_high = f.astype(BF).astype(F32)
            f_low = f - f_high
            left = jnp.concatenate(
                [
                    jnp.concatenate([f_high, f_high], axis=1),
                    jnp.concatenate([f_low, jnp.zeros_like(f_low)], axis=1),
                ],
                axis=0,
            ).astype(BF)
            right = jnp.concatenate([w_high, w_low], axis=1)
            o = lax.dot_general(left, right, (((1,), (1,)), ((), ())), preferred_element_type=F32)
            sums.append((block, o[0:8] + o[8:16]))
        for block, o in sums:
            acc_ref[block] += o
        return 0

    lax.fori_loop(0, lax.div(count + (UNROLL - 1), jnp.int32(UNROLL)), step, 0)


def match_kernel(blocks, place, length, spacing, first, last, codes_ref, count_ref, at_ref, *refs):
    refs = list(refs)
    if last:
        out_ref, prob_ref, acc_ref = refs[-3:]
        refs = refs[:-3]
    else:
        acc_ref = refs.pop()
    if first:
        acc_ref[...] = jnp.zeros_like(acc_ref)
    elif last:
        acc_ref[...] = refs.pop()[...]
    else:
        refs.pop()
    match_items(codes_ref, place * length, count_ref[place], spacing, at_ref, refs, acc_ref)
    if not last:
        return

    def finish(i, _):
        for t in range(8):
            block = i * 8 + t
            a = acc_ref[block]
            s = a[5:6]
            inverse = 1.0 / (1.0 + s)
            out_ref[:, pl.ds(pl.multiple_of(block * TB, TB), TB)] = (a * inverse)[0:5]
            prob_ref[pl.ds(block, 1), :] = s * inverse
        return 0

    lax.fori_loop(0, blocks // 8, finish, 0)


def match(blocks, place, length, spacing, last, codes, counts, at, arrays, acc):
    sums = jax.ShapeDtypeStruct((blocks + 1, 8, TB), F32)
    outs = (jax.ShapeDtypeStruct((5, blocks * TB), F32), jax.ShapeDtypeStruct((blocks, TB), F32))
    args = [codes, counts, at, *arrays] + ([] if acc is None else [acc])
    return pl.pallas_call(
        functools.partial(match_kernel, blocks, place, length, spacing, acc is None, last),
        out_shape=outs if last else sums,
        in_specs=[SMEM, SMEM] + [VMEM] * (len(args) - 2),
        out_specs=(VMEM, VMEM) if last else VMEM,
        scratch_shapes=[pltpu.VMEM(sums.shape, F32)] if last else [],
        input_output_aliases={} if last or acc is None else {len(args) - 1: 0},
        compiler_params=params(12),
        cost_estimate=pl.CostEstimate(flops=4 * 10**9, transcendentals=5 * 10**6, bytes_accessed=10**7),
    )(*args)


def work(a_coord, a_var, dest, cand, cand_count, b_coord, b_var, b_prior, b_flux):
    zones, tiles = lax.axis_size("zone"), lax.axis_size("tile")
    blocks = dest.shape[0]
    slots = cand.shape[1]
    own_blocks = b_var.shape[0] // TB
    rows = NQ * own_blocks
    fast = is_grid({"zone": zones, "tile": tiles})
    grid = Grid(zones, tiles)

    shift = (cand >= MB).astype(jnp.int32) + (cand >= MB + own_blocks).astype(jnp.int32) - 1
    zone = dest // tiles + shift
    tile = dest % tiles
    block = cand - MB - shift * own_blocks
    live = (jnp.arange(slots, dtype=jnp.int32)[None, :] < cand_count) & (zone >= 0) & (zone < zones)
    own = jnp.concatenate([b_coord, b_flux, b_var[None, :], b_prior[None, :]], axis=0).reshape(rows, TB)
    if fast:
        arrays, order = gather_phases(own, grid)
        phase, code = locate(zone, tile, block, grid, rows)
    else:
        arrays, order = [(lax.all_gather(own, AXES, axis=0, tiled=True),)], [0]
        phase, code = jnp.zeros_like(zone), (zone * tiles + tile) * rows + block
    phases = len(order)
    here = jnp.arange(blocks, dtype=jnp.int32)[:, None]
    entry = jnp.where(live, (phase << 27) | (here << 17) | code, phases << 27)
    items = blocks * slots
    length = items + UNROLL
    plan = pl.pallas_call(
        functools.partial(plan_kernel, phases, length, blocks << 17),
        out_shape=(
            jax.ShapeDtypeStruct(((phases + 1) * length,), jnp.int32),
            jax.ShapeDtypeStruct((8,), jnp.int32),
        ),
        in_specs=[VMEM],
        out_specs=(SMEM, SMEM),
        scratch_shapes=[
            pltpu.VMEM((2 * items // TB + 8, TB), jnp.int32),
            pltpu.SMEM((2 * items // TB + 8, TB), jnp.int32),
            pltpu.SemaphoreType.DMA(()),
        ],
        compiler_params=params(4),
        cost_estimate=pl.CostEstimate(flops=10**9, transcendentals=0, bytes_accessed=10**6),
        name="plan",
    )
    codes, counts = plan(entry.T.reshape(items // TB, TB))

    var_rows = a_var.reshape(blocks, TB)
    prep = pl.pallas_call(
        functools.partial(prep_kernel, blocks),
        out_shape=jax.ShapeDtypeStruct((blocks * TB, 48), BF),
        in_specs=[VMEM, VMEM],
        out_specs=VMEM,
        compiler_params=params(4),
        cost_estimate=pl.CostEstimate(flops=4 * 10**9, transcendentals=0, bytes_accessed=10**7),
        name="prep",
    )
    at = prep(a_coord, var_rows)
    at = pltpu.with_memory_space_constraint(at, pltpu.VMEM)

    acc = None
    for place, s in enumerate(order):
        last = place == phases - 1
        acc = match(blocks, s, length, own_blocks, last, codes, counts, at, arrays[place], acc)
    matched, prob = acc
    return matched, prob.reshape(-1)


def solution(mesh):
    placed = (
        P(None, AXES),
        P(AXES),
        P(AXES, None),
        P(AXES, None),
        P(AXES, None),
        P(None, AXES),
        P(AXES),
        P(AXES),
        P(None, AXES),
    )
    return jax.shard_map(work, mesh=mesh, in_specs=placed, out_specs=(P(None, AXES), P(AXES)), check_vma=False)
```

```python
import functools
import math

import jax
import jax.numpy as jnp
from jax import lax
from jax.experimental import pallas as pl
from jax.experimental.pallas import tpu as pltpu
from jax.sharding import PartitionSpec as P


TB = 128
MB = 8
NQ = 7
VAR, PRIOR = 5, 6
UNROLL = 32
BF, F32 = jnp.bfloat16, jnp.float32
HALF_LOG2E = 0.5 * math.log2(math.e)
AXES = ("zone", "tile")
VMEM = pl.BlockSpec(memory_space=pltpu.VMEM)
HBM = pl.BlockSpec(memory_space=pltpu.HBM)
SMEM = pl.BlockSpec(memory_space=pltpu.SMEM)


def params(mib):
    return pltpu.CompilerParams(vmem_limit_bytes=mib << 20)


def split3(x):
    high = x.astype(BF).astype(F32)
    middle = (x - high).astype(BF).astype(F32)
    return high, middle, x - high - middle


def is_grid(mesh_shape):
    return mesh_shape["zone"] % 2 == 0 and mesh_shape["tile"] == 4


class Grid:
    def __init__(self, zones, tiles):
        self.zones, self.tiles, self.high = zones, tiles, zones // 2

    def perm(self, move):
        pairs = []
        for d in range(self.zones * self.tiles):
            zone, tile = divmod(d, self.tiles)
            h, x, y, c = move(zone // 2, zone % 2, tile // 2, tile % 2)
            pairs.append((d, ((h % self.high) * 2 + x) * self.tiles + y * 2 + c))
        return pairs

    def shift(self, by):
        return self.perm(lambda h, x, y, c: (h + by, x, y, c))

    def side(self, first):
        return self.perm(lambda h, x, y, c: (h, x ^ 1, y, c) if (c == 0) == first else (h, x, y ^ 1, c))

    def core(self):
        return self.perm(lambda h, x, y, c: (h, x, y, c ^ 1))


def send(array, pairs):
    return lax.ppermute(array, AXES, pairs)


def gather_phases(own, grid):
    n = grid.high
    join = lambda parts: jnp.concatenate(parts, axis=0) if len(parts) > 1 else parts[0]
    up = down = join([own, send(own, grid.side(True))])
    phases = []
    for g in range(n // 2 + 1):
        pairs = [up]
        if g == 1:
            z = send(own, grid.shift(1))
            pairs = [join([z, send(z, grid.side(True))])]
        elif g > 1:
            pairs = [send(up, grid.shift(1))]
        if g > 0 and 2 * g != n:
            pairs.append(send(down, grid.shift(-1)))
        up, down = pairs[0], pairs[-1]
        near = join(pairs)
        across = send(near, grid.side(False))
        phases.append((near, across, send(near, grid.core()), send(across, grid.core())))
    return phases


def locate(zone, tile, block, grid, rows):
    my_zone, my_tile = lax.axis_index("zone"), lax.axis_index("tile")
    n = grid.high
    distance = (my_zone >> 1) - (zone >> 1)
    distance = jnp.where(distance < 0, distance + n, distance)
    phase = jnp.minimum(distance, n - distance)
    back = jnp.where(distance == phase, 0, 1)
    dx = (zone & 1) ^ (my_zone & 1)
    dy = ((tile >> 1) ^ (my_tile >> 1)) & 1
    dc = (tile ^ my_tile) & 1
    first = jnp.where((tile & 1) == 0, dx, dy)
    return phase, ((2 * dc + (dx + dy - first)) << 16) | ((2 * back + first) * rows + block)


def plan_kernel(grid, own_blocks, phases, length, *refs):
    *inputs, codes_ref, count_ref, dest_ref, cand_ref, live_ref, place_ref, work_ref, sems = refs
    copies = [
        pltpu.make_async_copy(a, b, sems.at[i]) for i, (a, b) in enumerate(zip(inputs, (dest_ref, cand_ref, live_ref)))
    ]
    for copy in copies:
        copy.start()
    for copy in copies:
        copy.wait()
    cand = cand_ref[...]
    _, blocks = cand.shape
    zones, tiles = grid.zones, grid.tiles
    rows = NQ * own_blocks
    dest = jnp.broadcast_to(dest_ref[...], cand.shape)
    home = jnp.zeros_like(cand)
    for z in range(1, zones):
        home = home + jnp.where(dest >= z * tiles, 1, 0)
    tile = dest - home * tiles
    shift = jnp.where(cand >= MB, 1, 0) + jnp.where(cand >= MB + own_blocks, 1, 0) - 1
    zone = home + shift
    block = cand - MB - shift * own_blocks
    slot = lax.broadcasted_iota(jnp.int32, cand.shape, 0)
    here = lax.broadcasted_iota(jnp.int32, cand.shape, 1)
    live = (slot < live_ref[...]) & (zone >= 0) & (zone < zones)
    if phases > 1:
        phase, code = locate(zone, tile, block, grid, rows)
    else:
        phase, code = jnp.zeros_like(zone), (zone * tiles + tile) * rows + block
    entry = jnp.where(live, (phase << 28) | (here << 18) | code, phases << 28)
    entry = jnp.concatenate([entry[:, g * TB : (g + 1) * TB] for g in range(blocks // TB)], axis=0)

    high = entry.shape[0]
    phase = entry >> 28
    lanes = (TB, TB)
    earlier = lax.broadcasted_iota(jnp.int32, lanes, 0) < lax.broadcasted_iota(jnp.int32, lanes, 1)
    sums = jnp.concatenate([jnp.where(earlier, 1.0, 0.0), jnp.ones(lanes, F32)], axis=1).astype(BF)
    above = lax.broadcasted_iota(jnp.int32, (high, high), 1) < lax.broadcasted_iota(jnp.int32, (high, high), 0)
    above = jnp.where(above, 1.0, 0.0).astype(BF)
    place = phase * length
    totals = []
    for p in range(phases + 1):
        member = jnp.where(phase == p, 1.0, 0.0)
        both = jnp.dot(member.astype(BF), sums, preferred_element_type=F32)
        before, total = both[:, :TB], both[:, TB:]
        ahead = jnp.dot(above, total.astype(BF), preferred_element_type=F32)
        place = place + jnp.where(phase == p, (before + ahead).astype(jnp.int32), 0)
        totals.append(jnp.sum(total, axis=0, keepdims=True).astype(jnp.int32))
    place_ref[pl.ds(0, high), :] = place
    place_ref[pl.ds(high, high), :] = entry & ((1 << 28) - 1)
    place_ref[pl.ds(2 * high, 8), :] = jnp.concatenate(
        totals + [jnp.zeros((1, TB), jnp.int32)] * (7 - phases), axis=0
    )
    copy = pltpu.make_async_copy(place_ref, work_ref, sems.at[3])
    copy.start()
    copy.wait()

    def row(r, _):
        for first in range(0, TB, 8):
            lanes = range(first, first + 8)
            places = [work_ref[r, t] for t in lanes]
            values = [work_ref[high + r, t] for t in lanes]
            for p, v in zip(places, values):
                codes_ref[p] = v
        return 0

    lax.fori_loop(0, high, row, 0)
    for p in range(phases):
        count_ref[p] = work_ref[2 * high + p, 0]


def prep_kernel(blocks, coord_ref, var_ref, at_ref):
    eye = jnp.where(
        lax.broadcasted_iota(jnp.int32, (TB, TB), 0) == lax.broadcasted_iota(jnp.int32, (TB, TB), 1), 1.0, 0.0
    ).astype(BF)
    row = lax.broadcasted_iota(jnp.int32, (8, TB), 0)

    def stack(block):
        lanes = pl.ds(pl.multiple_of(block * TB, TB), TB)
        u, v = coord_ref[0:1, lanes], coord_ref[1:2, lanes]
        s = var_ref[pl.ds(block, 1), :]
        q = -HALF_LOG2E * (u * u + v * v)
        tile = jnp.where(row == 3, q, jnp.where(row == 4, s, jnp.where(row == 2, 1.0, 0.0)))
        tile = jnp.where(row == 0, u, jnp.where(row == 1, v, tile))
        h, m, l = split3(tile)
        return [h, h, m, m, h, l]

    def step(i, _):
        for t in range(8):
            pair = i * 8 + t
            both = jnp.concatenate(stack(2 * pair) + stack(2 * pair + 1), axis=0).astype(BF)
            turned = lax.dot_general(eye, both, (((1,), (1,)), ((), ())), preferred_element_type=F32)
            at_ref[pl.ds(pl.multiple_of(pair * TB, TB), TB), :] = turned.astype(BF)
        return 0

    lax.fori_loop(0, blocks // 16, step, 0)


def match_items(codes_ref, first, count, dummy, spacing, at_ref, b_refs, acc_ref):
    row = lax.broadcasted_iota(jnp.int32, (8, TB), 0)
    gap = jnp.zeros((8 - NQ, TB), F32)

    def step(i, _):
        sums = []
        for t in range(UNROLL):
            item = i * UNROLL + t
            code = jnp.where(item < count, codes_ref[first + item], dummy)
            block, which, start = code >> 18, (code >> 16) & 3, code & 0xFFFF
            x = b_refs[0][pl.ds(start, NQ, stride=spacing), :]
            for k in range(1, len(b_refs)):
                x = jnp.where(which == k, b_refs[k][pl.ds(start, NQ, stride=spacing), :], x)
            x = jnp.concatenate([x, gap], axis=0)
            u, v, s, p = x[0:1], x[1:2], x[VAR : VAR + 1], x[PRIOR : PRIOR + 1]
            q = -HALF_LOG2E * (u * u + v * v)
            near = jnp.where(row == 2, q, jnp.where(row == 3, 1.0, 0.0))
            near = jnp.where(row < 2, x * (2 * HALF_LOG2E), near)
            spread = jnp.where(row == 2, s, jnp.where(row == 4, 1.0, 0.0))
            h, m, l = split3(jnp.concatenate([near, spread], axis=1))
            even = [jnp.where((block & 1) == 0, part, 0.0) for part in (h, m, l)]
            odd = [jnp.where((block & 1) == 0, 0.0, part) for part in (h, m, l)]
            stack = jnp.concatenate([a[k] for a in (even, odd) for k in (0, 1, 0, 1, 2, 0)], axis=0).astype(BF)
            held = jnp.minimum(block >> 1, at_ref.shape[0] // TB - 1)
            a = at_ref[pl.ds(pl.multiple_of(held * TB, TB), TB), :]
            both = jnp.dot(a, stack, preferred_element_type=F32)
            r = 1.0 / both[:, TB:]
            w = r * jnp.exp2(both[:, :TB] * r)
            w_high = w.astype(BF)
            w_low = (w - w_high.astype(F32)).astype(BF)
            f = jnp.where(row == VAR, 1.0, x) * (2.0 * p)
            f_high = f.astype(BF).astype(F32)
            f_low = f - f_high
            left = jnp.concatenate(
                [
                    jnp.concatenate([f_high, f_high], axis=1),
                    jnp.concatenate([f_low, jnp.zeros_like(f_low)], axis=1),
                ],
                axis=0,
            ).astype(BF)
            right = jnp.concatenate([w_high, w_low], axis=1)
            o = lax.dot_general(left, right, (((1,), (1,)), ((), ())), preferred_element_type=F32)
            sums.append((block, o[0:8] + o[8:16]))
        for block, o in sums:
            acc_ref[block] += o
        return 0

    lax.fori_loop(0, lax.div(count + (UNROLL - 1), jnp.int32(UNROLL)), step, 0)


def match_kernel(blocks, place, length, spacing, first, last, codes_ref, count_ref, at_ref, *refs):
    refs = list(refs)
    if last:
        out_ref, prob_ref, acc_ref = refs[-3:]
        refs = refs[:-3]
    else:
        acc_ref = refs.pop()
    if first:
        acc_ref[...] = jnp.zeros_like(acc_ref)
    elif last:
        acc_ref[...] = refs.pop()[...]
    else:
        refs.pop()
    match_items(codes_ref, place * length, count_ref[place], blocks << 18, spacing, at_ref, refs, acc_ref)
    if not last:
        return

    def finish(i, _):
        for t in range(8):
            block = i * 8 + t
            a = acc_ref[block]
            s = a[5:6]
            inverse = 1.0 / (1.0 + s)
            out_ref[:, pl.ds(pl.multiple_of(block * TB, TB), TB)] = (a * inverse)[0:5]
            prob_ref[pl.ds(block, 1), :] = s * inverse
        return 0

    lax.fori_loop(0, blocks // 8, finish, 0)


def match(blocks, place, length, spacing, last, codes, counts, at, arrays, acc):
    sums = jax.ShapeDtypeStruct((blocks + 1, 8, TB), F32)
    outs = (jax.ShapeDtypeStruct((5, blocks * TB), F32), jax.ShapeDtypeStruct((blocks, TB), F32))
    args = [codes, counts, at, *arrays] + ([] if acc is None else [acc])
    return pl.pallas_call(
        functools.partial(match_kernel, blocks, place, length, spacing, acc is None, last),
        out_shape=outs if last else sums,
        in_specs=[SMEM, SMEM] + [VMEM] * (len(args) - 2),
        out_specs=(VMEM, VMEM) if last else VMEM,
        scratch_shapes=[pltpu.VMEM(sums.shape, F32)] if last else [],
        input_output_aliases={} if last or acc is None else {len(args) - 1: 0},
        compiler_params=params(12),
        cost_estimate=pl.CostEstimate(flops=4 * 10**9, transcendentals=5 * 10**6, bytes_accessed=10**7),
    )(*args)


def work(a_coord, a_var, dest, cand, cand_count, b_coord, b_var, b_prior, b_flux):
    zones, tiles = lax.axis_size("zone"), lax.axis_size("tile")
    blocks = dest.shape[0]
    slots = cand.shape[1]
    own_blocks = b_var.shape[0] // TB
    rows = NQ * own_blocks
    fast = is_grid({"zone": zones, "tile": tiles})
    grid = Grid(zones, tiles)

    own = jnp.concatenate([b_coord, b_flux, b_var[None, :], b_prior[None, :]], axis=0).reshape(rows, TB)
    if fast:
        arrays = gather_phases(own, grid)
    else:
        arrays = [(lax.all_gather(own, AXES, axis=0, tiled=True),)]
    phases = len(arrays)
    items = blocks * slots
    length = items + UNROLL
    plan = pl.pallas_call(
        functools.partial(plan_kernel, grid, own_blocks, phases, length),
        out_shape=(
            jax.ShapeDtypeStruct(((phases + 1) * length,), jnp.int32),
            jax.ShapeDtypeStruct((8,), jnp.int32),
        ),
        in_specs=[HBM, HBM, HBM],
        out_specs=(SMEM, SMEM),
        scratch_shapes=[
            pltpu.VMEM((1, blocks), jnp.int32),
            pltpu.VMEM((slots, blocks), jnp.int32),
            pltpu.VMEM((1, blocks), jnp.int32),
            pltpu.VMEM((2 * items // TB + 8, TB), jnp.int32),
            pltpu.SMEM((2 * items // TB + 8, TB), jnp.int32),
            pltpu.SemaphoreType.DMA((4,)),
        ],
        compiler_params=params(4),
        cost_estimate=pl.CostEstimate(flops=10**9, transcendentals=0, bytes_accessed=10**6),
        name="plan",
    )
    codes, counts = plan(*(pltpu.with_memory_space_constraint(x.T, pltpu.HBM) for x in (dest, cand, cand_count)))

    var_rows = a_var.reshape(blocks, TB)
    prep = pl.pallas_call(
        functools.partial(prep_kernel, blocks),
        out_shape=jax.ShapeDtypeStruct((blocks // 2 * TB, 96), BF),
        in_specs=[VMEM, VMEM],
        out_specs=VMEM,
        compiler_params=params(4),
        cost_estimate=pl.CostEstimate(flops=4 * 10**9, transcendentals=0, bytes_accessed=10**7),
        name="prep",
    )
    at = prep(a_coord, var_rows)
    at = pltpu.with_memory_space_constraint(at, pltpu.VMEM)

    acc = None
    for place in range(phases):
        last = place == phases - 1
        acc = match(blocks, place, length, own_blocks, last, codes, counts, at, arrays[place], acc)
    matched, prob = acc
    return matched, prob.reshape(-1)


def solution(mesh):
    placed = (
        P(None, AXES),
        P(AXES),
        P(AXES, None),
        P(AXES, None),
        P(AXES, None),
        P(None, AXES),
        P(AXES),
        P(AXES),
        P(None, AXES),
    )
    return jax.shard_map(work, mesh=mesh, in_specs=placed, out_specs=(P(None, AXES), P(AXES)), check_vma=False)
```
